32 devices in a mesh: dp: 8 (over z, y), tensor: 4 (over x, core).
Axes of the slice: x: 2, y: 2, z: 4, core: 2. Of those that a mesh axis runs over, the one named last changes fastest.
Arguments:
- tokens: bfloat16 [4096, 2048], P(('dp', 'tensor')), may hold values from -6 to 6
- cotangent: bfloat16 [4096, 2048], P(('dp', 'tensor')), may hold values from -6 to 6
- valid_mask: int32 [4096], P(('dp', 'tensor')), may hold values 0 or 1
- seq_lengths: int32 [4], replicated, may hold values from 1 to 2048, 4096 in all
- block_order: int32 [32], replicated, may hold values from 0 to 31, each once
- norm_gain1: float32 [2048], P(('dp', 'tensor')), may hold values from 0.5 to 1.5
- w_input: bfloat16 [2048, 2048], P('dp', 'tensor'), may hold values from -0.125 to 0.125
- w_forget: bfloat16 [2048, 2048], P('dp', 'tensor'), may hold values from -0.125 to 0.125
- w_gate_mix: bfloat16 [2048, 2048], P('dp', 'tensor'), may hold values from -0.125 to 0.125
- forget_bias: float32 [2048], P(('dp', 'tensor')), may hold values from -2 to 8
- out_gain: float32 [2048], P(('dp', 'tensor')), may hold values from 0.5 to 1.5
- w_out: bfloat16 [2048, 2048], P('tensor', 'dp'), may hold values from -0.1875 to 0.1875
- norm_gain2: float32 [2048], P(('dp', 'tensor')), may hold values from 0.5 to 1.5
- w_gate: bfloat16 [2048, 5632], P('dp', 'tensor'), may hold values from -0.125 to 0.125
- w_up: bfloat16 [2048, 5632], P('dp', 'tensor'), may hold values from -0.125 to 0.125
- w_down: bfloat16 [5632, 2048], P('tensor', 'dp'), may hold values from -0.15625 to 0.15625
Outputs:
- layer_out: bfloat16 [4096, 2048], P(('dp', 'tensor'))
- input_grad: bfloat16 [4096, 2048], P(('dp', 'tensor'))
- grad_norm_gain1: float32 [2048], P(('dp', 'tensor'))
- grad_w_input: float32 [2048, 2048], P('dp', 'tensor')
- grad_w_forget: float32 [2048, 2048], P('dp', 'tensor')
- grad_w_gate_mix: float32 [2048, 2048], P('dp', 'tensor')
- grad_forget_bias: float32 [2048], P(('dp', 'tensor'))
- grad_out_gain: float32 [2048], P(('dp', 'tensor'))
- grad_w_out: float32 [2048, 2048], P('tensor', 'dp')
- grad_norm_gain2: float32 [2048], P(('dp', 'tensor'))
- grad_w_gate: float32 [2048, 5632], P('dp', 'tensor')
- grad_w_up: float32 [2048, 5632], P('dp', 'tensor')
- grad_w_down: float32 [5632, 2048], P('tensor', 'dp')
- rms_stats: float32 [3], replicated
The draws below stay inside these ranges and needn't reach their ends.
Inputs may be any that keep to these rules, and one draw needn't show every extreme that they name: `seq_lengths`: 4 packed sequences in pack order that cover all 4096 tokens; the longest has exactly 2048 tokens. `block_order`: entry j names the block of 128 pack tokens held by dealt block j; every block once.
All inputs are finite; a program needn't handle non-finite values. No bound on the sum of `valid_mask` on one device may be relied on, other than what follows from the above.
Results may differ from the reference program's by a relative error of at most 0.0095.
Values may be sent and summed in bfloat16 or wider, within the bound.
A program may use at most 192 MiB of HBM per device.

```python
import math
import jax
import jax.numpy as jnp
import numpy as np
from jax import lax

D = 2048
FF = 5632
BLOCK = 128
TOKENS = 4096
NBLK = 32
MAXLEN = 2048
NSEQ = 4
N_DP = 8


def with_ends(array, own_key, low, top_value):
    shape = array.shape
    place = [jax.random.randint(jax.random.fold_in(own_key, axis), (), 0, shape[axis]) for axis in range(len(shape))]
    array = array.at[tuple(place)].set(low)
    longest = shape.index(max(shape))
    place[longest] = (place[longest] + 1) % shape[longest]
    return array.at[tuple(place)].set(top_value)


def block_scale(own_key, shape, cuts, smallest, top_value):
    def one(position, shards_of):
        draws = jax.random.uniform(jax.random.fold_in(jax.random.fold_in(own_key, 6), position), (shards_of,), jnp.float32, smallest / len(cuts), top_value / len(cuts))
        return jnp.repeat(jnp.exp(draws), shape[position] // shards_of).reshape((-1,) + (1,) * (len(shape) - position - 1))

    loudness = one(*cuts[0])
    for cut in cuts[1:]:
        loudness = loudness * one(*cut)
    return loudness


def split_up(count, total, most, skew):
    weights = [(1 << 20) // math.isqrt(grade ** skew) + 1 for grade in range(2, count + 1)]
    spare, counts = total - most - (count - 1), [1] * (count - 1)
    while spare > 0:
        movable = [i for i in range(count - 1) if counts[i] < most]
        pool, budget = sum([weights[i] for i in movable]), spare
        for i in movable:
            addition = min(most - counts[i], max(1, budget * weights[i] // pool), spare)
            counts[i] = counts[i] + addition
            spare = spare - addition
    return np.array([most] + counts)


def uneven_parts(key, number_of, total, limit, slope):
    if number_of == 2:
        one = jax.random.randint(key, (), max(1, total - limit), min(limit, total - 1) + 1)
        return jnp.stack([one, total - one])
    lengths = jnp.asarray(split_up(number_of, total, limit, slope), jnp.int32)
    twos = (number_of - 1) // 2
    donor, receiver = lengths[1:1 + 2 * twos:2], lengths[2:2 + 2 * twos:2]
    slack = jnp.minimum(donor - 1, limit - receiver)
    shifted = jax.random.randint(jax.random.fold_in(key, 1), (twos,), 0, 1 << 20) % (slack + 1)
    lengths = lengths.at[1:1 + 2 * twos:2].set(donor - shifted).at[2:2 + 2 * twos:2].set(receiver + shifted)
    return lengths[jax.random.permutation(jax.random.fold_in(key, 2), number_of)]


def centred(own_key, dims, width, reach, cuts=(), kind=jnp.bfloat16):
    drawn = jax.random.normal(own_key, dims, jnp.float32) * width
    if len(cuts) > 0:
        drawn = block_scale(own_key, dims, cuts, -0.22, 0.18) * drawn
    return jnp.clip(drawn, min=-reach, max=reach).astype(kind)


def setup_inputs(seed: int = 0) -> dict:
    seeds = jax.random.split(jax.random.key(seed), 17)
    tokens = centred(seeds[0], (TOKENS, D), 1.0, 6.0, ((0, 32),))
    cotangent = centred(seeds[1], (TOKENS, D), 1.0, 6.0, ((0, 32),))
    valid_mask = with_ends((jax.random.randint(seeds[2], (TOKENS,), 0, 8) < 7).astype(jnp.int32), jax.random.fold_in(seeds[2], 1), 0, 1)
    seq_lengths = uneven_parts(seeds[3], NSEQ, TOKENS, MAXLEN, 2).astype(jnp.int32)
    block_order = jax.random.permutation(seeds[4], NBLK).astype(jnp.int32)
    norm_gain1 = jnp.clip(1.0 + 0.1 * jax.random.normal(seeds[5], (D,), jnp.float32), 0.5, 1.5)
    w_input = centred(seeds[6], (D, D), D ** -0.5, 0.125, ((0, 8), (1, 4)))
    w_forget = centred(seeds[7], (D, D), D ** -0.5, 0.125, ((0, 8), (1, 4)))
    w_gate_mix = centred(seeds[8], (D, D), D ** -0.5, 0.125, ((0, 8), (1, 4)))
    forget_bias = jnp.clip(-2.0 + 10.0 * jax.random.uniform(seeds[9], (D,), jnp.float32) ** block_scale(seeds[9], (D,), ((0, 32),), -0.2, 0.2), -2.0, 8.0)
    out_gain = jnp.clip(1.0 + 0.1 * jax.random.normal(seeds[10], (D,), jnp.float32), 0.5, 1.5)
    w_out = centred(seeds[11], (D, D), (D // 2) ** -0.5, 0.1875, ((0, 4), (1, 8)))
    norm_gain2 = jnp.clip(1.0 + 0.1 * jax.random.normal(seeds[12], (D,), jnp.float32), 0.5, 1.5)
    w_gate = centred(seeds[13], (D, FF), D ** -0.5, 0.125, ((0, 8), (1, 4)))
    w_up = centred(seeds[14], (D, FF), D ** -0.5, 0.125, ((0, 8), (1, 4)))
    w_down = centred(seeds[15], (FF, D), (FF // 4) ** -0.5, 0.15625, ((0, 4), (1, 8)))
    return dict(tokens=tokens, cotangent=cotangent, valid_mask=valid_mask, seq_lengths=seq_lengths, block_order=block_order, norm_gain1=norm_gain1, w_input=w_input, w_forget=w_forget, w_gate_mix=w_gate_mix, forget_bias=forget_bias, out_gain=out_gain, w_out=w_out, norm_gain2=norm_gain2, w_gate=w_gate, w_up=w_up, w_down=w_down)


epsilon = 1e-06
lower_bound = 0.75

@jax.custom_vjp
def low(v):
    return lax.optimization_barrier(v.astype(jnp.bfloat16)).astype(jnp.float32)

@jax.custom_vjp
def low_back(v):
    return v

def low_keep(v):
    return (low(v), None)

def low_pass(kept, grad):
    return (grad,)

def back_keep(v):
    return (v, None)

def back_low(kept, grad):
    return (low(grad),)
low.defvjp(low_keep, low_pass)
low_back.defvjp(back_keep, back_low)

def matmul(operand, matrix):
    return jnp.dot(operand, matrix, precision=lax.Precision.HIGHEST, preferred_element_type=jnp.float32)

def rms_norm(values, gain_vector):
    return values * lax.rsqrt(lax.optimization_barrier(jnp.mean(values * values, axis=1, keepdims=True)) + epsilon) * gain_vector

def reference(tokens, cotangent, valid_mask, seq_lengths, block_order, norm_gain1, w_input, w_forget, w_gate_mix, forget_bias, out_gain, w_out, norm_gain2, w_gate, w_up, w_down):
    offsets = jnp.arange(BLOCK, dtype=jnp.int32)
    source_rows = (block_order[:, None] * BLOCK + offsets[None, :]).reshape(-1).astype(jnp.int32)
    inverse = jnp.zeros((TOKENS,), jnp.int32).at[source_rows].set(jnp.arange(TOKENS, dtype=jnp.int32))
    seq_starts = (jnp.cumsum(seq_lengths) - seq_lengths).astype(jnp.int32)
    start_flags = jnp.any(jnp.arange(TOKENS, dtype=jnp.int32)[:, None] == seq_starts[None, :], axis=1)
    keep_flag = jnp.where(start_flags[source_rows], 0.0, 1.0).astype(jnp.float32)[:, None]
    valid_rows = valid_mask.astype(jnp.float32)

    def forward(stream, gain_first, weight_input, weight_forget, weight_mix, bias_forget, gain_out, weight_out, gain_second, weight_gate, weight_up, weight_down):

        def first_half(row_block):
            normed = low(rms_norm(row_block, gain_first))
            input_raw = low_back(matmul(normed, weight_input))
            forget_raw = low_back(matmul(normed, weight_forget))
            gate_raw = low_back(matmul(normed, weight_mix))
            forget_gate = lower_bound + (1.0 - lower_bound) * jax.nn.sigmoid(forget_raw + bias_forget)
            increment = jax.nn.silu(input_raw) * (1.0 - forget_gate)
            return (forget_gate, increment, gate_raw)
        parts = lax.map(jax.checkpoint(first_half), stream.reshape(N_DP, -1, D))
        forget_gate = parts[0].reshape(TOKENS, D)
        increment = parts[1].reshape(TOKENS, D)
        gate_raw = parts[2].reshape(TOKENS, D)
        decay_rate = forget_gate * keep_flag

        def advance(carry_state, step_pair):
            new_state = step_pair[0] * carry_state + step_pair[1]
            return (new_state, new_state)
        final_state, states_packed = lax.scan(advance, jnp.zeros((D,), jnp.float32), (decay_rate[inverse], increment[inverse]))
        hidden_state = states_packed[source_rows]

        def second_half(block_tuple):
            row_block, state_block, gate_block = block_tuple
            state_normed = state_block * lax.rsqrt(lax.optimization_barrier(jnp.mean(state_block * state_block, axis=1, keepdims=True)) + epsilon)
            mixed = low(state_normed * gain_out * jax.nn.silu(gate_block))
            mixer_out = low_back(matmul(mixed, weight_out))
            after = row_block + mixer_out
            normed = low(rms_norm(after, gain_second))
            gate_pre = low_back(matmul(normed, weight_gate))
            up_pre = low_back(matmul(normed, weight_up))
            hidden_units = low(jax.nn.silu(gate_pre) * up_pre)
            ffn_out = low_back(matmul(hidden_units, weight_down))
            return (after + ffn_out, mixer_out, ffn_out)
        results = lax.map(jax.checkpoint(second_half), (stream.reshape(N_DP, -1, D), hidden_state.reshape(N_DP, -1, D), gate_raw.reshape(N_DP, -1, D)))
        return (results[0].reshape(TOKENS, D), (results[1].reshape(TOKENS, D), results[2].reshape(TOKENS, D)))
    params = (norm_gain1, w_input, w_forget, w_gate_mix, forget_bias, out_gain, w_out, norm_gain2, w_gate, w_up, w_down)
    params = tuple((item.astype(jnp.float32) for item in params))
    residual_sum, pull_back, branch_outs = jax.vjp(forward, tokens.astype(jnp.float32), *params, has_aux=True)
    gradients = pull_back(cotangent.astype(jnp.float32) * valid_rows[:, None])
    divisor = jnp.maximum(jnp.sum(valid_rows), 1.0) * D

    def root_mean(values):
        return jnp.sqrt(jnp.sum(valid_rows[:, None] * values * values) / divisor)
    rms_stats = jnp.stack([root_mean(residual_sum), root_mean(branch_outs[0]), root_mean(branch_outs[1])])
    return (residual_sum.astype(jnp.bfloat16), gradients[0].astype(jnp.bfloat16), gradients[1], gradients[2], gradients[3], gradients[4], gradients[5], gradients[6], gradients[7], gradients[8], gradients[9], gradients[10], gradients[11], rms_stats)
```

```python
import functools

import jax
import jax.numpy as jnp
from jax import lax
from jax.experimental import pallas as pl
from jax.experimental.pallas import tpu as pltpu
from jax.sharding import PartitionSpec as P

D = 2048
BLOCK = 128
MESH = pl.DeviceIdType.MESH

epsilon = 1e-06
lower_bound = 0.75
TILE = 8


def row_scale(values):
    return lax.rsqrt(jnp.mean(values * values, axis=1, keepdims=True) + epsilon)


def dot(operand, matrix):
    return jnp.dot(operand, matrix, preferred_element_type=jnp.float32)


def times_transposed(operand, matrix):
    return lax.dot_general(
        operand, matrix, (((1,), (1,)), ((), ())), preferred_element_type=jnp.float32
    )


def inner_rows(operand, matrix):
    return lax.dot_general(
        operand, matrix, (((0,), (0,)), ((), ())), preferred_element_type=jnp.float32
    )


def silu_slope(values, sigmoid_value):
    return sigmoid_value * (1.0 + values * (1.0 - sigmoid_value))


def norm_back(grad_normed, scaled_rows, row_factor, gain_vector):
    grad_scaled = grad_normed * gain_vector
    mean_term = jnp.mean(grad_scaled * scaled_rows, axis=1, keepdims=True)
    return (
        row_factor * (grad_scaled - scaled_rows * mean_term),
        jnp.sum(grad_normed * scaled_rows, axis=0),
    )


def widen(values, channel_start):
    return lax.dynamic_update_slice_in_dim(jnp.zeros((D,), jnp.float32), values, channel_start, 0)


def tensor_rows(values):
    return lax.all_gather(values, "tensor", axis=0, tiled=True)


def tensor_reduce(partial_term):
    return lax.psum_scatter(
        partial_term.astype(jnp.bfloat16), "tensor", scatter_dimension=0, tiled=True
    ).astype(jnp.float32)


def flat_exchange_kernel(dp, tp, reduce, x_ref, out_ref, held, send_sem, recv_sem):
    count = dp * tp
    me = lax.axis_index("dp") * tp + lax.axis_index("tensor")
    barrier = pltpu.get_barrier_semaphore()

    def place(k):
        peer = lax.rem(me + k, count)
        return peer, (lax.div(peer, tp), lax.rem(peer, tp))

    def greet(k, carry):
        _, where = place(k)
        pl.semaphore_signal(barrier, inc=1, device_id=where, device_id_type=MESH)
        return carry

    lax.fori_loop(1, count, greet, 0)
    held[pl.ds(me, 1)] = x_ref[pl.ds(me if reduce else 0, 1)]
    pl.semaphore_wait(barrier, count - 1)

    def send(k, carry):
        peer, where = place(k)
        pltpu.make_async_remote_copy(
            src_ref=x_ref.at[pl.ds(peer if reduce else 0, 1)],
            dst_ref=held.at[pl.ds(me, 1)],
            send_sem=send_sem,
            recv_sem=recv_sem,
            device_id=where,
            device_id_type=MESH,
        ).start()
        return carry

    lax.fori_loop(1, count, send, 0)
    rows = held.at[pl.ds(0, count - 1)]
    pltpu.make_async_copy(rows, rows, send_sem).wait()
    pltpu.make_async_copy(rows, rows, recv_sem).wait()
    if reduce:
        out_ref[...] = jnp.sum(held[...], axis=0, keepdims=True)
    else:
        out_ref[...] = held[...]


def flat_exchange(x, dp, tp, reduce):
    count = dp * tp
    return pl.pallas_call(
        functools.partial(flat_exchange_kernel, dp, tp, reduce),
        out_shape=jax.ShapeDtypeStruct((1 if reduce else count, 8, 128), jnp.float32),
        in_specs=[pl.BlockSpec(memory_space=pltpu.VMEM)],
        out_specs=pl.BlockSpec(memory_space=pltpu.VMEM),
        scratch_shapes=[
            pltpu.VMEM((count, 8, 128), jnp.float32),
            pltpu.SemaphoreType.DMA,
            pltpu.SemaphoreType.DMA,
        ],
        compiler_params=pltpu.CompilerParams(
            collective_id=1 if reduce else 0, has_side_effects=True
        ),
        cost_estimate=pl.CostEstimate(flops=0, bytes_accessed=16 << 20, transcendentals=0),
        name="flat_reduce" if reduce else "flat_gather",
    )(x)


def carry_kernel(dp, reverse, ends_ref, rows_ref, ids_ref, out_ref, held, entering, send_sem, recv_sem):
    me = lax.axis_index("dp")
    barrier = pltpu.get_barrier_semaphore()
    height = ends_ref.shape[0]
    here = height // 2
    blocks = rows_ref.shape[0]

    def greet(k, carry):
        pl.semaphore_signal(
            barrier, inc=1, device_id={"dp": lax.rem(me + k, dp)}, device_id_type=MESH
        )
        return carry

    lax.fori_loop(1, dp, greet, 0)
    own = pl.ds(pl.multiple_of(me * height, height), height)
    held[own, :] = ends_ref[...]
    pl.semaphore_wait(barrier, dp - 1)

    def send(k, carry):
        pltpu.make_async_remote_copy(
            src_ref=ends_ref,
            dst_ref=held.at[own],
            send_sem=send_sem,
            recv_sem=recv_sem,
            device_id={"dp": lax.rem(me + k, dp)},
            device_id_type=MESH,
        ).start()
        return carry

    lax.fori_loop(1, dp, send, 0)
    rows = held.at[pl.ds(0, (dp - 1) * height)]
    pltpu.make_async_copy(rows, rows, send_sem).wait()
    pltpu.make_async_copy(rows, rows, recv_sem).wait()

    def step(i, state):
        p = blocks - 1 - i if reverse else i
        entering[pl.ds(p, 1), :] = state
        row = rows_ref[p]
        return held[pl.ds(row, 1), :] * state + held[pl.ds(row + here, 1), :]

    lax.fori_loop(0, blocks, step, jnp.zeros((1, ends_ref.shape[1]), jnp.float32))
    for b in range(here):
        out_ref[pl.ds(b, 1), :] = entering[pl.ds(ids_ref[b], 1), :]


def block_carry(ends, pack_rows, block_ids, dp, reverse):
    height, width = ends.shape
    blocks = pack_rows.shape[0]
    return pl.pallas_call(
        functools.partial(carry_kernel, dp, reverse),
        out_shape=jax.ShapeDtypeStruct((height // 2, width), jnp.float32),
        in_specs=[
            pl.BlockSpec(memory_space=pltpu.VMEM),
            pl.BlockSpec(memory_space=pltpu.SMEM),
            pl.BlockSpec(memory_space=pltpu.SMEM),
        ],
        out_specs=pl.BlockSpec(memory_space=pltpu.VMEM),
        scratch_shapes=[
            pltpu.VMEM((dp * height, width), jnp.float32),
            pltpu.VMEM((blocks, width), jnp.float32),
            pltpu.SemaphoreType.DMA,
            pltpu.SemaphoreType.DMA,
        ],
        compiler_params=pltpu.CompilerParams(
            collective_id=3 if reverse else 2, has_side_effects=True
        ),
        cost_estimate=pl.CostEstimate(flops=0, bytes_accessed=16 << 20, transcendentals=0),
        name="carry_back" if reverse else "carry_fwd",
    )(ends, pack_rows, block_ids)


def scan_kernel(input_ref, forget_ref, bias_ref, keep_ref, cum_ref, local_ref, ends_ref):
    width = input_ref.shape[1]
    here = input_ref.shape[0] // BLOCK
    line = lax.broadcasted_iota(jnp.int32, (TILE, width), 0)

    def tile_step(i, carry):
        out = []
        for b in range(here):
            rows = pl.ds(pl.multiple_of(b * BLOCK + i * TILE, TILE), TILE)
            forget = lower_bound + (1.0 - lower_bound) * lax.logistic(forget_ref[rows, :] + bias_ref[...])
            raw = input_ref[rows, :]
            total = raw * lax.logistic(raw) * (1.0 - forget)
            decay = forget * keep_ref[rows, :]
            for shift in (1, 2, 4):
                ahead = line >= shift
                before_total = pltpu.roll(total, shift, 0)
                before_decay = pltpu.roll(decay, shift, 0)
                total = jnp.where(ahead, decay * before_total + total, total)
                decay = jnp.where(ahead, decay * before_decay, decay)
            far_decay, far_total = carry[2 * b], carry[2 * b + 1]
            total = decay * far_total + total
            decay = decay * far_decay
            cum_ref[rows, :] = decay
            local_ref[rows, :] = total
            out += [decay[TILE - 1 :, :], total[TILE - 1 :, :]]
        return tuple(out)

    start = (jnp.ones((1, width), jnp.float32), jnp.zeros((1, width), jnp.float32)) * here
    last = lax.fori_loop(0, BLOCK // TILE, tile_step, start)
    for b in range(here):
        ends_ref[pl.ds(b, 1), :] = last[2 * b]
        ends_ref[pl.ds(here + b, 1), :] = last[2 * b + 1]


def local_scan(input_raw, forget_raw, bias, keep):
    rows, width = input_raw.shape
    full = jax.ShapeDtypeStruct((rows, width), jnp.float32)
    return pl.pallas_call(
        scan_kernel,
        out_shape=(full, full, jax.ShapeDtypeStruct((2 * (rows // BLOCK), width), jnp.float32)),
        in_specs=[pl.BlockSpec(memory_space=pltpu.VMEM)] * 4,
        out_specs=(pl.BlockSpec(memory_space=pltpu.VMEM),) * 3,
        cost_estimate=pl.CostEstimate(flops=0, bytes_accessed=12 << 20, transcendentals=0),
        name="scan_fwd",
    )(input_raw, forget_raw, bias, keep)


def scan_back_kernel(grad_ref, forget_ref, bias_ref, keep_ref, decay_ref, total_ref, ends_ref):
    width = grad_ref.shape[1]
    here = grad_ref.shape[0] // BLOCK
    tiles = BLOCK // TILE
    line = lax.broadcasted_iota(jnp.int32, (TILE, width), 0)

    def tile_step(i, carry):
        out = []
        for b in range(here):
            rows = pl.ds(pl.multiple_of(b * BLOCK + (tiles - 1 - i) * TILE, TILE), TILE)
            forget = lower_bound + (1.0 - lower_bound) * lax.logistic(forget_ref[rows, :] + bias_ref[...])
            own_decay = forget * keep_ref[rows, :]
            next_decay, far_decay, far_total = carry[3 * b : 3 * b + 3]
            decay = jnp.where(line == TILE - 1, next_decay, pltpu.roll(own_decay, TILE - 1, 0))
            total = grad_ref[rows, :]
            for shift in (1, 2, 4):
                behind = line < TILE - shift
                after_total = pltpu.roll(total, TILE - shift, 0)
                after_decay = pltpu.roll(decay, TILE - shift, 0)
                total = jnp.where(behind, decay * after_total + total, total)
                decay = jnp.where(behind, decay * after_decay, decay)
            total = decay * far_total + total
            decay = decay * far_decay
            decay_ref[rows, :] = decay
            total_ref[rows, :] = total
            out += [own_decay[:1, :], decay[:1, :], total[:1, :]]
        return tuple(out)

    one = jnp.ones((1, width), jnp.float32)
    last = lax.fori_loop(0, tiles, tile_step, (one, one, jnp.zeros_like(one)) * here)
    for b in range(here):
        ends_ref[pl.ds(b, 1), :] = last[3 * b] * last[3 * b + 1]
        ends_ref[pl.ds(here + b, 1), :] = last[3 * b] * last[3 * b + 2]


def local_scan_back(grad_direct, forget_raw, bias, keep):
    rows, width = grad_direct.shape
    full = jax.ShapeDtypeStruct((rows, width), jnp.float32)
    return pl.pallas_call(
        scan_back_kernel,
        out_shape=(full, full, jax.ShapeDtypeStruct((2 * (rows // BLOCK), width), jnp.float32)),
        in_specs=[pl.BlockSpec(memory_space=pltpu.VMEM)] * 4,
        out_specs=(pl.BlockSpec(memory_space=pltpu.VMEM),) * 3,
        cost_estimate=pl.CostEstimate(flops=0, bytes_accessed=12 << 20, transcendentals=0),
        name="scan_back",
    )(grad_direct, forget_raw, bias, keep)


def gate_back_kernel(
    decay_ref, total_ref, back_ref, cum_ref, local_ref, carry_ref, input_ref, forget_ref, bias_ref, keep_ref,
    grad_input_ref, grad_forget_ref, grad_bias_ref,
):
    b = pl.program_id(0)
    state_grad = total_ref[...] + decay_ref[...] * back_ref[pl.ds(b, 1), :]
    entering = carry_ref[pl.ds(b, 1), :]
    hidden = local_ref[...] + cum_ref[...] * entering
    line = lax.broadcasted_iota(jnp.int32, hidden.shape, 0)
    before = jnp.where(line == 0, entering, pltpu.roll(hidden, 1, 0))
    sigma = lax.logistic(forget_ref[...] + bias_ref[...])
    forget = lower_bound + (1.0 - lower_bound) * sigma
    raw = input_ref[...]
    input_sigma = lax.logistic(raw)
    grad_forget = keep_ref[...] * state_grad * before - state_grad * (raw * input_sigma)
    grad_pre = grad_forget * (1.0 - lower_bound) * sigma * (1.0 - sigma)
    grad_forget_ref[...] = grad_pre.astype(jnp.bfloat16)
    grad_input_ref[...] = (state_grad * (1.0 - forget) * silu_slope(raw, input_sigma)).astype(jnp.bfloat16)

    @pl.when(b == 0)
    def _():
        grad_bias_ref[...] = jnp.zeros_like(grad_bias_ref)

    grad_bias_ref[...] += jnp.sum(grad_pre, axis=0, keepdims=True)


def gate_back(tail_decay, tail_grad, carry_back, cum, local, carry_in, input_raw, forget_raw, bias, keep):
    rows, width = input_raw.shape
    here = rows // BLOCK
    tall = pl.BlockSpec((BLOCK, width), lambda b: (b, 0))
    small = pl.BlockSpec((here, width), lambda b: (0, 0))
    line = pl.BlockSpec((1, width), lambda b: (0, 0))
    half = jax.ShapeDtypeStruct((rows, width), jnp.bfloat16)
    return pl.pallas_call(
        gate_back_kernel,
        grid=(here,),
        out_shape=(half, half, jax.ShapeDtypeStruct((1, width), jnp.float32)),
        in_specs=[tall, tall, small, tall, tall, small, tall, tall, line, pl.BlockSpec((BLOCK, 1), lambda b: (b, 0))],
        out_specs=(tall, tall, line),
        cost_estimate=pl.CostEstimate(flops=0, bytes_accessed=12 << 20, transcendentals=0),
        name="gate_back",
    )(tail_decay, tail_grad, carry_back, cum, local, carry_in, input_raw, forget_raw, bias, keep)


class Plain:
    def __init__(self, dp):
        self.dp = dp

    def to_slots(self, values):
        return values

    def from_slots(self, values):
        return values

    def gather(self, shard, mode):
        return (lax.all_gather(shard, "dp", axis=0, tiled=True),)

    def reduce(self, rows, cols, mode):
        partial_sum = inner_rows(rows[0], cols).astype(jnp.bfloat16)
        return lax.psum_scatter(partial_sum, "dp", scatter_dimension=0, tiled=True).astype(jnp.float32)

    def split(self, values):
        return (values,)


class Chain:
    def __init__(self, dp, window=2):
        self.dp = dp
        self.length = dp // 2
        index = lax.axis_index("dp")
        self.pos = lax.div(index, 2)
        self.pair = lax.rem(index, 2)
        self.block = D // dp
        self.window = window
        self.history = {"up": [], "down": [], "pair": []}

    def send(self, lane, values, pairs):
        past = self.history[lane]
        if len(past) >= self.window:
            values, _ = lax.optimization_barrier((values, past[-self.window]))
        arrived = lax.ppermute(values, "dp", pairs)
        past.append(arrived)
        return arrived

    def up(self, values, first, last):
        return self.send("up", values, [(2 * z + y, 2 * z + 2 + y) for z in range(first, last + 1) for y in range(2)])

    def down(self, values, first, last):
        return self.send("down", values, [(2 * z + y, 2 * z - 2 + y) for z in range(first, last + 1) for y in range(2)])

    def swap(self, values):
        return self.send("pair", values, [(i, i ^ 1) for i in range(self.dp)])

    def to_slots(self, values):
        places = []
        for other in range(2):
            for r in range(self.length):
                start = (lax.rem(self.pos + self.length - r, self.length) * 2 + (self.pair ^ other)) * self.block
                places.append(lax.dynamic_slice_in_dim(values, start, self.block, values.ndim - 1))
        return jnp.concatenate(places, axis=-1)

    def from_slots(self, values):
        places = []
        for z in range(self.length):
            for y in range(2):
                start = ((self.pair ^ y) * self.length + lax.rem(self.pos + self.length - z, self.length)) * self.block
                places.append(lax.dynamic_slice_in_dim(values, start, self.block, values.ndim - 1))
        return jnp.concatenate(places, axis=-1)

    def spread(self, piece):
        n = self.length
        ups, downs = [piece], [piece]
        for r in range(1, n):
            ups.append(self.up(ups[-1], r - 1, n - 2))
            downs.append(self.down(downs[-1], 1, n - r))
        return [piece] + [jnp.where(self.pos >= r, ups[r], downs[n - r]) for r in range(1, n)]

    def collect(self, slots):
        n = self.length
        term = lambda r, arrived: (slots[r] + arrived.astype(jnp.float32)).astype(jnp.bfloat16)
        up, down = slots[1].astype(jnp.bfloat16), slots[n - 1].astype(jnp.bfloat16)
        for k in range(1, n):
            up_in = self.up(up, 0, min(k - 1, n - 2))
            down_in = self.down(down, max(n - k, 1), n - 1)
            if k < n - 1:
                up, down = term(k + 1, up_in), term(n - 1 - k, down_in)
        return slots[0] + up_in.astype(jnp.float32) + down_in.astype(jnp.float32)

    def gather(self, shard, mode):
        rows = shard.shape[0]
        if mode == "chain first":
            own = jnp.concatenate(self.spread(shard), axis=0)
            return own, self.swap(own)
        both = jnp.stack([shard, self.swap(shard)])
        slots = self.spread(both)
        return (
            jnp.concatenate([s[0] for s in slots], axis=0),
            jnp.concatenate([s[1] for s in slots], axis=0),
        )

    def reduce(self, rows, cols, mode):
        own_rows, other_rows = rows
        n, size = self.length, self.block
        other = inner_rows(other_rows, cols).astype(jnp.bfloat16)
        if mode == "chain first":
            own = inner_rows(own_rows, cols).astype(jnp.bfloat16)
            halves = [v.reshape(n, 1, size, -1) for v in (own, other)]
            both = [jnp.concatenate([h[r] for h in halves], axis=0).astype(jnp.float32) for r in range(n)]
            total = self.collect(both)
            return total[0] + self.swap(total[1].astype(jnp.bfloat16)).astype(jnp.float32)
        arrived = self.swap(other).reshape(n, size, -1)
        own = inner_rows(own_rows, cols).astype(jnp.bfloat16).reshape(n, size, -1)
        return self.collect([own[r].astype(jnp.float32) + arrived[r].astype(jnp.float32) for r in range(n)])

    def split(self, values):
        return values[:, : D // 2], values[:, D // 2 :]


def across(operand_parts, weight_parts):
    total = dot(operand_parts[0], weight_parts[0])
    for operand, weight in zip(operand_parts[1:], weight_parts[1:]):
        total = total + dot(operand, weight)
    return total


def back_across(terms):
    count = len(terms[0][1])
    columns = []
    for i in range(count):
        total = times_transposed(terms[0][0], terms[0][1][i])
        for operand, parts in terms[1:]:
            total = total + times_transposed(operand, parts[i])
        columns.append(total.astype(jnp.bfloat16))
    return columns[0] if count == 1 else jnp.concatenate(columns, axis=1)


def shards(
    dp,
    tp,
    tokens,
    cotangent,
    valid_mask,
    seq_lengths,
    block_order,
    norm_gain1,
    w_input,
    w_forget,
    w_gate_mix,
    forget_bias,
    out_gain,
    w_out,
    norm_gain2,
    w_gate,
    w_up,
    w_down,
):
    count = dp * tp
    dp_index = lax.axis_index("dp")
    tensor_index = lax.axis_index("tensor")
    own_rows = tokens.shape[0]
    group_rows = own_rows * tp
    blocks_here = group_rows // BLOCK
    width_local = w_input.shape[1]
    channel_start = tensor_index * width_local
    lanes = Chain(dp) if dp == 8 else Plain(dp)

    small_width = norm_gain1.shape[0]
    packed = jnp.concatenate([norm_gain1, forget_bias, out_gain, norm_gain2])
    packed = jnp.pad(packed, (0, 1024 - packed.shape[0])).reshape(1, 8, 128)
    gathered = flat_exchange(packed, dp, tp, False).reshape(count, 1024)[:, : 4 * small_width]
    gathered = gathered.reshape(count, 4, small_width)
    gain_first = lanes.to_slots(gathered[:, 0].reshape(1, D))
    bias_local = lax.dynamic_slice_in_dim(gathered[:, 1].reshape(1, D), channel_start, width_local, 1)
    gain_out = lax.dynamic_slice_in_dim(gathered[:, 2].reshape(1, D), channel_start, width_local, 1)
    gain_second = lanes.to_slots(gathered[:, 3].reshape(1, D))

    mixer_cat = jnp.concatenate([w_input, w_forget, w_gate_mix], axis=1)
    mixer_parts = lanes.gather(mixer_cat, "chain first")
    out_parts = lanes.gather(w_out.T, "chain first")
    gate_parts = lanes.gather(w_gate, "chain first")
    up_parts = lanes.gather(w_up, "chain first")
    down_parts = lanes.gather(w_down.T, "pair first")

    block_ids = lax.dynamic_slice_in_dim(block_order, dp_index * blocks_here, blocks_here)
    positions = block_ids[:, None] * BLOCK + jnp.arange(BLOCK, dtype=jnp.int32)[None, :]
    seq_starts = jnp.cumsum(seq_lengths) - seq_lengths
    is_start = jnp.any(positions[:, :, None] == seq_starts[None, None, :], axis=2)
    keep_flag = jnp.where(is_start, 0.0, 1.0).astype(jnp.float32).reshape(group_rows, 1)
    every = jnp.arange(block_order.shape[0], dtype=jnp.int32)
    dealt = jnp.sum(jnp.where(block_order[None, :] == every[:, None], every[None, :], 0), axis=1)
    pack_rows = dealt + (dealt // blocks_here) * blocks_here

    stream = lanes.to_slots(tokens).astype(jnp.float32)
    scale_first = row_scale(stream)
    scaled_first = stream * scale_first
    mixer_in = tensor_rows((scaled_first * gain_first).astype(jnp.bfloat16))
    mixer_in_parts = lanes.split(mixer_in)
    mixer_raw = [
        across(mixer_in_parts, [p[:, i * width_local : (i + 1) * width_local] for p in mixer_parts])
        for i in range(3)
    ]
    input_raw, forget_raw, gate_raw = mixer_raw
    cum_decay, local_state, ends = local_scan(input_raw, forget_raw, bias_local, keep_flag)
    carry_in = block_carry(ends, pack_rows, block_ids, dp, False)

    def blocks(values):
        return values.reshape(blocks_here, BLOCK, width_local)

    hidden_state = (blocks(local_state) + blocks(cum_decay) * carry_in[:, None, :]).reshape(group_rows, width_local)
    square_total = lax.psum(jnp.sum(hidden_state * hidden_state, axis=1), "tensor")
    state_scale = lax.rsqrt(square_total / D + epsilon)[:, None]
    state_normed = hidden_state * state_scale
    gate_sigma = jax.nn.sigmoid(gate_raw)
    gate_act = gate_raw * gate_sigma
    mixer_cast = (state_normed * gain_out * gate_act).astype(jnp.bfloat16)
    mixer_out = tensor_reduce(back_across([(mixer_cast, out_parts)]))
    after_mixer = stream + mixer_out

    scale_second = row_scale(after_mixer)
    scaled_second = after_mixer * scale_second
    ffn_in = tensor_rows((scaled_second * gain_second).astype(jnp.bfloat16))
    ffn_in_parts = lanes.split(ffn_in)
    gate_pre = across(ffn_in_parts, gate_parts)
    up_pre = across(ffn_in_parts, up_parts)
    gate_sig = jax.nn.sigmoid(gate_pre)
    hidden_units = (gate_pre * gate_sig * up_pre).astype(jnp.bfloat16)

    valid_rows = valid_mask.astype(jnp.float32)
    grad_out = lanes.to_slots(cotangent).astype(jnp.float32) * valid_rows[:, None]
    grad_ffn_all = tensor_rows(grad_out.astype(jnp.bfloat16))
    grad_ffn_parts = lanes.split(grad_ffn_all)
    grad_down = lanes.reduce(grad_ffn_parts, hidden_units, "pair first")
    grad_hidden = across(grad_ffn_parts, down_parts)
    grad_gate_pre = (grad_hidden * up_pre * silu_slope(gate_pre, gate_sig)).astype(jnp.bfloat16)
    grad_up_pre = (grad_hidden * gate_pre * gate_sig).astype(jnp.bfloat16)
    grad_gate = lanes.reduce(ffn_in_parts, grad_gate_pre, "pair first")
    grad_up = lanes.reduce(ffn_in_parts, grad_up_pre, "pair first")
    grad_normed_second = tensor_reduce(back_across([(grad_gate_pre, gate_parts), (grad_up_pre, up_parts)]))
    ffn_out = tensor_reduce(back_across([(hidden_units, down_parts)]))
    residual_sum = after_mixer + ffn_out
    grad_stream_second, grad_gain_second = norm_back(
        grad_normed_second, scaled_second, scale_second, gain_second
    )
    grad_after = grad_out + grad_stream_second

    grad_mix_all = tensor_rows(grad_after.astype(jnp.bfloat16))
    grad_mix_parts = lanes.split(grad_mix_all)
    grad_mixed = across(grad_mix_parts, out_parts)
    grad_wout = lanes.reduce(grad_mix_parts, mixer_cast, "pair first")
    grad_gain_out_local = jnp.sum(grad_mixed * state_normed * gate_act, axis=0)
    grad_gate_raw = (
        grad_mixed * state_normed * gain_out * silu_slope(gate_raw, gate_sigma)
    ).astype(jnp.bfloat16)
    grad_normed_state = grad_mixed * gain_out * gate_act
    cross_total = lax.psum(jnp.sum(grad_normed_state * state_normed, axis=1), "tensor")
    grad_direct = state_scale * (grad_normed_state - state_normed * (cross_total / D)[:, None])
    tail_decay, tail_grad, head = local_scan_back(grad_direct, forget_raw, bias_local, keep_flag)
    carry_back = block_carry(head, pack_rows, block_ids, dp, True)
    grad_input_raw, grad_forget_raw, grad_bias_local = gate_back(
        tail_decay, tail_grad, carry_back, cum_decay, local_state, carry_in, input_raw, forget_raw, bias_local, keep_flag
    )
    grad_wmix = lanes.reduce(mixer_in_parts, grad_gate_raw, "pair first")
    grad_winput = lanes.reduce(mixer_in_parts, grad_input_raw, "pair first")
    grad_wforget = lanes.reduce(mixer_in_parts, grad_forget_raw, "pair first")
    mixer_back = [
        (g, [p[:, i * width_local : (i + 1) * width_local] for p in mixer_parts])
        for i, g in enumerate((grad_input_raw, grad_forget_raw, grad_gate_raw))
    ]
    grad_normed_first = tensor_reduce(back_across(mixer_back))
    grad_stream_first, grad_gain_first = norm_back(
        grad_normed_first, scaled_first, scale_first, gain_first
    )
    input_grad = lanes.from_slots((grad_after + grad_stream_first).astype(jnp.bfloat16))
    layer_out = lanes.from_slots(residual_sum.astype(jnp.bfloat16))

    totals = jnp.stack(
        [
            jnp.sum(valid_rows * jnp.sum(residual_sum * residual_sum, axis=1)),
            jnp.sum(valid_rows * jnp.sum(mixer_out * mixer_out, axis=1)),
            jnp.sum(valid_rows * jnp.sum(ffn_out * ffn_out, axis=1)),
            jnp.sum(valid_rows),
        ]
    )
    small_terms = [
        lanes.from_slots(grad_gain_first.reshape(1, D)),
        widen(grad_bias_local[0], channel_start),
        widen(grad_gain_out_local, channel_start),
        lanes.from_slots(grad_gain_second.reshape(1, D)),
    ]
    outgoing = jnp.concatenate(
        [term.reshape(count, small_width) for term in small_terms]
        + [jnp.broadcast_to(totals[None, :], (count, 4)), jnp.zeros((count, 1020 - 4 * small_width), jnp.float32)],
        axis=1,
    )
    summed = flat_exchange(outgoing.reshape(count, 8, 128), dp, tp, True).reshape(1024)
    small_summed = summed[: 4 * small_width].reshape(4, small_width)
    totals = summed[4 * small_width : 4 * small_width + 4]
    rms_stats = jnp.sqrt(totals[:3] / (jnp.maximum(totals[3], 1.0) * D))
    return (
        layer_out,
        input_grad,
        small_summed[0],
        grad_winput,
        grad_wforget,
        grad_wmix,
        small_summed[1],
        small_summed[2],
        grad_wout.T,
        small_summed[3],
        grad_gate,
        grad_up,
        grad_down.T,
        rms_stats,
    )


def solution(mesh):
    rows = P(("dp", "tensor"), None)
    flat = P(("dp", "tensor"))
    first, second = P("dp", "tensor"), P("tensor", "dp")
    return jax.shard_map(
        functools.partial(shards, mesh.shape["dp"], mesh.shape["tensor"]),
        mesh=mesh,
        in_specs=(
            rows, rows, flat, P(), P(), flat, first, first, first, flat, flat, second, flat, first, first, second,
        ),
        out_specs=(
            rows, rows, flat, first, first, first, flat, flat, second, flat, first, first, second, P(),
        ),
        check_vma=False,
    )
```
